32 devices in a mesh: grp: 8 (over z, x), nbr: 4 (over y, core).
Axes of the slice: x: 2, y: 2, z: 4, core: 2. Of those that a mesh axis runs over, the one named last changes fastest.
Arguments:
- gains: float32 [128, 256, 256], P(('grp', 'nbr')), may hold values from -1 to 1
- covs: float32 [128, 256, 256], P(('grp', 'nbr')), may hold values from -10 to 10, as said below
- terminal: float32 [256, 256], replicated, may hold values from -4 to 4, as said below
Outputs:
- smoothed: float32 [128, 256, 256], P(('grp', 'nbr'))
The draws below stay inside these ranges and needn't reach their ends.
Inputs may be any that keep to these rules, and one draw needn't show every extreme that they name: `covs`: each matrix is symmetric positive definite. `terminal`: symmetric positive definite.
All inputs are finite; a program needn't handle non-finite values.
Results may differ from the reference program's by a relative error of at most 0.0003.
Values sent between devices are 32-bit elements; how exact they have to be, the bound alone decides.
A program may use at most 64 MiB of HBM per device.

```python
import math
import jax
import jax.numpy as jnp
from jax import lax

STATE_SIZE = 256
TIME_STEPS = 128


def draw_gains(key, part):
    random_keys = jax.random.split(jax.random.fold_in(key, 11), 5)
    raw = jax.random.normal(random_keys[0], (TIME_STEPS, STATE_SIZE, STATE_SIZE), jnp.float32) * (0.25 / math.sqrt(STATE_SIZE))
    skew = raw - jnp.swapaxes(raw, 1, 2)
    identity_matrix = jnp.eye(STATE_SIZE, dtype=jnp.float32)
    rotate = jnp.linalg.solve(identity_matrix[None] - skew, identity_matrix[None] + skew)
    share = 1.0 / 8.0
    fast = jax.random.uniform(random_keys[1], (STATE_SIZE,)) < share
    fast_rate = jax.random.uniform(random_keys[2], (STATE_SIZE,), minval=1.0 / 50.0, maxval=1.0 / 30.0)
    rate = jnp.where(fast, fast_rate, 0.5 / TIME_STEPS)
    jitter = jax.random.uniform(random_keys[3], (TIME_STEPS, STATE_SIZE), minval=0.6, maxval=1.4)
    scale_factor = jnp.exp(-rate[None, :] * jitter)
    device_places = jax.random.randint(random_keys[4], (4,), 0, TIME_STEPS)
    sample_group = jnp.any(jnp.arange(TIME_STEPS)[:, None] == device_places[None, :], axis=1)
    scale_factor = scale_factor * jnp.where(sample_group, 0.75, 1.0)[:, None]
    return (scale_factor[:, :, None] * rotate).astype(jnp.float32)


def draw_covs(key, part):
    random_keys = jax.random.split(jax.random.fold_in(key, 23), 2)
    process_noise = jax.random.normal(random_keys[0], (TIME_STEPS, STATE_SIZE, STATE_SIZE), jnp.float32)
    inner_product = jnp.einsum('kij,klj->kil', process_noise, process_noise) / STATE_SIZE
    extra_term = jax.random.uniform(random_keys[1], (TIME_STEPS, STATE_SIZE), minval=0.5, maxval=1.5)
    square_matrix = inner_product + extra_term[:, :, None] * jnp.eye(STATE_SIZE, dtype=jnp.float32)[None]
    return (0.01 * square_matrix).astype(jnp.float32)


def draw_terminal(key, part):
    random_keys = jax.random.split(jax.random.fold_in(key, 37), 2)
    process_noise = jax.random.normal(random_keys[0], (STATE_SIZE, STATE_SIZE), jnp.float32)
    extra_term = jax.random.uniform(random_keys[1], (STATE_SIZE,), minval=0.5, maxval=1.5)
    return (0.5 * jnp.dot(process_noise, process_noise.T) / STATE_SIZE + jnp.diag(extra_term)).astype(jnp.float32)


def setup_inputs(seed: int = 0) -> dict:
    key_of = jax.random.split(jax.random.key(seed), 4)
    gains = draw_gains(jax.random.fold_in(key_of[3], 71), 0)
    covs = draw_covs(jax.random.fold_in(key_of[3], 71), 0)
    terminal = draw_terminal(jax.random.fold_in(key_of[3], 71), 0)
    return dict(gains=gains, covs=covs, terminal=terminal)


def reference(gains, covs, terminal):

    def advance(state, pair):
        gain, cov = pair
        left = jnp.dot(gain.astype(jnp.float32), state.astype(jnp.float32), precision=lax.Precision.HIGHEST, preferred_element_type=jnp.float32)
        nxt = lax.dot_general(left.astype(jnp.float32), gain.astype(jnp.float32), (((1,), (1,)), ((), ())), precision=lax.Precision.HIGHEST, preferred_element_type=jnp.float32) + cov
        return (nxt, nxt)
    _, result = lax.scan(advance, terminal, (gains, covs), reverse=True)
    return result
```

```python
import functools

import jax
import jax.numpy as jnp
from jax import lax
from jax.experimental import pallas as pl
from jax.experimental.pallas import tpu as pltpu
from jax.sharding import PartitionSpec as P

MESH = pl.DeviceIdType.MESH
F32, BF16 = jnp.float32, jnp.bfloat16
NN = (((1,), (0,)), ((), ()))
NT = (((1,), (1,)), ((), ()))


def halves(a):
    high = a.astype(BF16)
    return high, (a - high.astype(F32)).astype(BF16)


def left_form(a):
    high, low = halves(a)
    return jnp.concatenate([high, high, low], axis=1)


def right_form(b):
    high, low = halves(b)
    return jnp.concatenate([high, low, high], axis=0)


def right_form_tr(b):
    high, low = halves(b)
    return jnp.concatenate([high, low, high], axis=1)


def product(a, b):
    return lax.dot_general(a, b, NN, preferred_element_type=F32)


def product_tr(a, b):
    return lax.dot_general(a, b, NT, preferred_element_type=F32)


def congruence(gain, cov, state):
    mixed = product(left_form(gain), right_form(state))
    return product_tr(left_form(mixed), right_form_tr(gain)) + cov


def compose(first, second):
    gain = product(left_form(first[0]), right_form(second[0]))
    return gain, congruence(first[0], first[1], second[1])


def tree(pairs):
    while len(pairs) > 1:
        nxt = [compose(pairs[i], pairs[i + 1]) for i in range(0, len(pairs) - 1, 2)]
        if len(pairs) % 2:
            nxt.append(pairs[-1])
        pairs = nxt
    return pairs[0]


def kernel(groups, nbrs, g_ref, c_ref, t_ref, o_ref, tot, suf, loc, fin, state, out_state, beyond, ssem, rsem):
    count, width = g_ref.shape[0], g_ref.shape[1]
    half = width // 2
    quarter_len = groups // 4
    g, n = lax.axis_index("grp"), lax.axis_index("nbr")
    core = lax.rem(n, 2)
    quarter = g // quarter_len
    mate = (g, n + 1 - 2 * core)
    mine = pl.ds(pl.multiple_of(core * half, half), half)

    levels = []
    step = 1
    while step < nbrs:
        bit = lax.rem(n // step, 2)
        levels.append((bit, (g, n + step * (1 - 2 * bit))))
        step *= 2
    step = 1
    while step < quarter_len:
        bit = lax.rem(g // step, 2)
        levels.append((bit, (g + step * (1 - 2 * bit), n)))
        step *= 2
    down = (lax.rem(g + 3 * quarter_len, groups), n)
    up = (lax.rem(g + quarter_len, groups), n)

    barrier = pltpu.get_barrier_semaphore()
    greeted = [partner for _, partner in levels] + [down, up]
    for other in greeted:
        pl.semaphore_signal(barrier, inc=1, device_id=other, device_id_type=MESH)

    sems = iter(range(ssem.shape[0]))

    def copy(src, dst, to, sem):
        return pltpu.make_async_remote_copy(
            src_ref=src, dst_ref=dst, send_sem=ssem.at[sem], recv_sem=rsem.at[sem],
            device_id=to, device_id_type=MESH,
        )

    first_bit = levels[0][0]
    pairs = [(g_ref[k], c_ref[k]) for k in range(count)]
    gain, cov = tree(pairs)
    tot[0, first_bit, 0] = gain
    tot[0, first_bit, 1] = cov
    pl.semaphore_wait(barrier, len(greeted))

    pending = []
    for at, (bit, partner) in enumerate(levels):
        moved, passed = [], []
        for part in range(2):
            sem = next(sems)
            if at == 0:
                ref = tot.at[at, bit, part]
                moved.append(copy(ref, ref, partner, sem))
            else:
                ref = tot.at[at, bit, part, mine]
                moved.append(copy(ref, ref, partner, sem))
                sem = next(sems)
                ref = tot.at[at, 1 - bit, part, mine]
                passed.append(copy(ref, ref, mate, sem))
        for one in moved:
            one.start()
        if at == 0:
            own = (g_ref[count - 1], c_ref[count - 1])
            for k in range(count - 1, 0, -1):
                if k < count - 1:
                    own = compose((g_ref[k], c_ref[k]), own)
                loc[k, 0], loc[k, 1] = own
            loc[0, 0], loc[0, 1] = tot[0, first_bit, 0], tot[0, first_bit, 1]
            rows = lax.broadcasted_iota(jnp.int32, (width, width), 0)
            columns = lax.broadcasted_iota(jnp.int32, (width, width), 1)
            suf[0] = jnp.where(rows == columns, F32(1), F32(0))
            suf[1] = jnp.zeros((width, width), F32)
        else:
            @pl.when(levels[at - 1][0] == 0)
            def _():
                new = compose((suf[0], suf[1]), (tot[at - 1, 1, 0], tot[at - 1, 1, 1]))
                suf[0], suf[1] = new
        for i, one in enumerate(moved):
            one.wait_recv()
            if passed:
                passed[i].start()
        if passed:
            for one in passed:
                one.wait_recv()
        pending += moved + passed
        new = compose((tot[at, 0, 0], tot[at, 0, 1]), (tot[at, 1, 0], tot[at, 1, 1]))
        slot = levels[at + 1][0] if at + 1 < len(levels) else 0
        tot[at + 1, slot, 0], tot[at + 1, slot, 1] = new

    last = len(levels)
    total = tot.at[last, 0]

    pair_sems = [next(sems) for _ in range(4)]
    state_sem, state_pass_sem = next(sems), next(sems)
    send_pair = [copy(total.at[i, mine], beyond.at[i, mine], down, pair_sems[i]) for i in range(2)]
    pass_pair = [copy(beyond.at[i, mine], beyond.at[i, mine], mate, pair_sems[2 + i]) for i in range(2)]
    send_state = copy(out_state.at[mine], state.at[mine], down, state_sem)
    relay_state = copy(state.at[mine], state.at[mine], down, state_sem)
    pass_state = copy(state.at[mine], state.at[mine], mate, state_pass_sem)

    def finish_suffix():
        @pl.when(levels[-1][0] == 0)
        def _():
            new = compose((suf[0], suf[1]), (tot[last - 1, 1, 0], tot[last - 1, 1, 1]))
            suf[0], suf[1] = new

    def finals():
        for k in range(count):
            new = compose((loc[k, 0], loc[k, 1]), (suf[0], suf[1]))
            fin[k, 0], fin[k, 1] = new

    @pl.when(quarter == 3)
    def _():
        out_state[...] = congruence(total[0], total[1], t_ref[...])
        send_state.start()
        state[...] = t_ref[...]
        finish_suffix()
        finals()
        send_state.wait_send()

    @pl.when(quarter == 2)
    def _():
        finish_suffix()
        send_state.wait_recv()
        pass_state.start()
        pass_state.wait_recv()
        out_state[...] = congruence(total[0], total[1], state[...])
        send_state.start()
        finals()
        pass_state.wait_send()
        send_state.wait_send()

    @pl.when(quarter == 1)
    def _():
        for one in send_pair:
            one.start()
        finish_suffix()
        finals()
        relay_state.wait_recv()
        relay_state.start()
        pass_state.start()
        pass_state.wait()
        for one in send_pair:
            one.wait_send()
        relay_state.wait_send()

    @pl.when(quarter == 0)
    def _():
        finish_suffix()
        for i, one in enumerate(send_pair):
            one.wait_recv()
            pass_pair[i].start()
        for one in pass_pair:
            one.wait()
        suf[0], suf[1] = compose((suf[0], suf[1]), (beyond[0], beyond[1]))
        finals()
        relay_state.wait_recv()
        pass_state.start()
        pass_state.wait()

    entering = right_form(state[...])
    for k in range(count):
        mixed = product(left_form(fin[k, 0]), entering)
        o_ref[k] = product_tr(left_form(mixed), right_form_tr(fin[k, 0])) + fin[k, 1]

    for one in pending:
        one.wait_send()


def solution(mesh):
    groups, nbrs = mesh.shape["grp"], mesh.shape["nbr"]
    levels = (nbrs.bit_length() - 1) + ((groups // 4).bit_length() - 1)
    n_sems = 2 + 4 * (levels - 1) + 6

    def per_device(gains, covs, terminal):
        count, width = gains.shape[0], gains.shape[1]
        pair = (2, width, width)
        vmem = pl.BlockSpec(memory_space=pltpu.VMEM)
        return pl.pallas_call(
            functools.partial(kernel, groups, nbrs),
            out_shape=jax.ShapeDtypeStruct(gains.shape, F32),
            in_specs=[vmem] * 3,
            out_specs=vmem,
            scratch_shapes=[
                pltpu.VMEM((levels + 1, 2) + pair, F32),
                pltpu.VMEM(pair, F32),
                pltpu.VMEM((count,) + pair, F32),
                pltpu.VMEM((count,) + pair, F32),
                pltpu.VMEM((width, width), F32),
                pltpu.VMEM((width, width), F32),
                pltpu.VMEM(pair, F32),
                pltpu.SemaphoreType.DMA((n_sems,)),
                pltpu.SemaphoreType.DMA((n_sems,)),
            ],
            compiler_params=pltpu.CompilerParams(collective_id=0, has_side_effects=True),
        )(gains, covs, terminal)

    placed = P(("grp", "nbr"), None, None)
    return jax.shard_map(
        per_device, mesh=mesh, in_specs=(placed, placed, P()), out_specs=placed, check_vma=False
    )
```

```python
import functools

import jax
import jax.numpy as jnp
from jax import lax
from jax.experimental import pallas as pl
from jax.experimental.pallas import tpu as pltpu
from jax.sharding import PartitionSpec as P

MESH = pl.DeviceIdType.MESH
F32, BF16 = jnp.float32, jnp.bfloat16
PAD = 8
NN = (((1,), (0,)), ((), ()))
NT = (((1,), (1,)), ((), ()))


def halves(a):
    high = a.astype(BF16)
    return high, (a - high.astype(F32)).astype(BF16)


def left_form(a):
    high, low = halves(a)
    return jnp.concatenate([high, high, low], axis=1)


def right_form(b):
    high, low = halves(b)
    return jnp.concatenate([high, low, high], axis=0)


def right_form_tr(b):
    high, low = halves(b)
    return jnp.concatenate([high, low, high], axis=1)


def product(a, b):
    return lax.dot_general(a, b, NN, preferred_element_type=F32)


def product_tr(a, b):
    return lax.dot_general(a, b, NT, preferred_element_type=F32)


def congruence(gain, cov, state):
    mixed = product(left_form(gain), right_form(state))
    return product_tr(left_form(mixed), right_form_tr(gain)) + cov


def compose(first, second):
    gain = product(left_form(first[0]), right_form(second[0]))
    return gain, congruence(first[0], first[1], second[1])


def tree(pairs):
    while len(pairs) > 1:
        nxt = [compose(pairs[i], pairs[i + 1]) for i in range(0, len(pairs) - 1, 2)]
        if len(pairs) % 2:
            nxt.append(pairs[-1])
        pairs = nxt
    return pairs[0]


def symmetric_masks(half):
    rows = lax.broadcasted_iota(jnp.int32, (half, half), 0)
    columns = lax.broadcasted_iota(jnp.int32, (half, half), 1)
    return rows <= columns, rows == columns


def pack(ref, full):
    half = full.shape[0] // 2
    upper, diagonal = symmetric_masks(half)
    a, b, c = full[:half, :half], full[:half, half:], full[half:, half:]
    ref[0, pl.ds(0, half)] = b
    ref[1, pl.ds(0, half)] = jnp.where(upper, a, c)
    line = jnp.sum(jnp.where(diagonal, c, F32(0)), axis=0, keepdims=True)
    line = jnp.broadcast_to(line, (PAD, half))
    ref[0, pl.ds(half, PAD)] = line
    ref[1, pl.ds(half, PAD)] = line


def unpack(ref):
    half = ref.shape[2]
    upper, diagonal = symmetric_masks(half)
    b, mixed = ref[0, pl.ds(0, half)], ref[1, pl.ds(0, half)]
    line = ref[0, pl.ds(half, 1)]
    mixed_tr = mixed.T
    a = jnp.where(upper, mixed, mixed_tr)
    c = jnp.where(diagonal, line, jnp.where(upper, mixed_tr, mixed))
    return jnp.concatenate(
        [jnp.concatenate([a, b], axis=1), jnp.concatenate([b.T, c], axis=1)], axis=0
    )


def kernel(
    groups, nbrs, g_ref, c_ref, t_ref, o_ref,
    tot_e, tot_l, full_l, suf, loc, fin, state, out_state, beyond_e, beyond_l, ssem, rsem,
):
    count, width = g_ref.shape[0], g_ref.shape[1]
    half = width // 2
    quarter_len = groups // 4
    g, n = lax.axis_index("grp"), lax.axis_index("nbr")
    core = lax.rem(n, 2)
    quarter = g // quarter_len
    mate = (g, n + 1 - 2 * core)
    mine = pl.ds(pl.multiple_of(core * half, half), half)

    levels = []
    step = 1
    while step < nbrs:
        bit = lax.rem(n // step, 2)
        levels.append((bit, (g, n + step * (1 - 2 * bit))))
        step *= 2
    step = 1
    while step < quarter_len:
        bit = lax.rem(g // step, 2)
        levels.append((bit, (g + step * (1 - 2 * bit), n)))
        step *= 2
    last = len(levels)
    down = (lax.rem(g + 3 * quarter_len, groups), n)
    up = (lax.rem(g + quarter_len, groups), n)

    barrier = pltpu.get_barrier_semaphore()
    greeted = [partner for _, partner in levels] + [down, up]
    for other in greeted:
        pl.semaphore_signal(barrier, inc=1, device_id=other, device_id_type=MESH)

    sems = iter(range(ssem.shape[0]))

    def copy(src, dst, to, sem):
        return pltpu.make_async_remote_copy(
            src_ref=src, dst_ref=dst, send_sem=ssem.at[sem], recv_sem=rsem.at[sem],
            device_id=to, device_id_type=MESH,
        )

    plan = []
    for at, (bit, partner) in enumerate(levels):
        moves = []
        for ref, piece in ((tot_e, mine), (tot_l, core)):
            if at == 0:
                out = ref.at[at, bit]
                moves.append((copy(out, out, partner, next(sems)), None))
            else:
                out, came = ref.at[at, bit, piece], ref.at[at, 1 - bit, piece]
                moves.append((copy(out, out, partner, next(sems)), copy(came, came, mate, next(sems))))
        plan.append(moves)

    pending = []

    def start(move):
        move[0].start()
        pending.append(move[0])

    def arrive(move):
        move[0].wait_recv()
        if move[1] is not None:
            move[1].start()
            pending.append(move[1])
            move[1].wait_recv()

    def slot_of(at):
        return levels[at][0] if at < last else 0

    def put_cov(at, cov):
        full_l[at, slot_of(at)] = cov
        if at < last:
            pack(tot_l.at[at, slot_of(at)], cov)

    gain, cov = tree([(g_ref[k], c_ref[k]) for k in range(count)])
    tot_e[0, slot_of(0)] = gain
    put_cov(0, cov)
    pl.semaphore_wait(barrier, len(greeted))
    start(plan[0][0])
    start(plan[0][1])

    def extend_suffix(at):
        @pl.when(levels[at][0] == 0)
        def _():
            new = compose((suf[0], suf[1]), (tot_e[at, 1], full_l[at, 1]))
            suf[0], suf[1] = new

    for at, (bit, _) in enumerate(levels):
        arrive(plan[at][0])
        first = left_form(tot_e[at, 0])
        tot_e[at + 1, slot_of(at + 1)] = product(first, right_form(tot_e[at, 1]))
        if at + 1 < last:
            start(plan[at + 1][0])
        arrive(plan[at][1])
        full_l[at, 1 - bit] = unpack(tot_l.at[at, 1 - bit])
        put_cov(at + 1, congruence(tot_e[at, 0], full_l[at, 0], full_l[at, 1]))
        if at + 1 < last:
            start(plan[at + 1][1])
            if at == 0:
                own = (g_ref[count - 1], c_ref[count - 1])
                for k in range(count - 1, 0, -1):
                    if k < count - 1:
                        own = compose((g_ref[k], c_ref[k]), own)
                    loc[k, 0], loc[k, 1] = own
                loc[0, 0], loc[0, 1] = tot_e[0, slot_of(0)], full_l[0, slot_of(0)]
                rows = lax.broadcasted_iota(jnp.int32, (width, width), 0)
                columns = lax.broadcasted_iota(jnp.int32, (width, width), 1)
                suf[0] = jnp.where(rows == columns, F32(1), F32(0))
                suf[1] = jnp.zeros((width, width), F32)
            extend_suffix(at)

    total_e, total_l = tot_e.at[last, 0], full_l.at[last, 0]

    send_gain = copy(total_e.at[mine], beyond_e.at[mine], down, next(sems))
    send_cov = copy(out_state.at[core], beyond_l.at[core], down, next(sems))
    pass_gain = copy(beyond_e.at[mine], beyond_e.at[mine], mate, next(sems))
    pass_cov = copy(beyond_l.at[core], beyond_l.at[core], mate, next(sems))
    state_sem, pass_sem = next(sems), next(sems)
    send_state = copy(out_state.at[core], state.at[core], down, state_sem)
    relay_state = copy(state.at[core], state.at[core], down, state_sem)
    pass_state = copy(state.at[core], state.at[core], mate, pass_sem)

    def finals():
        for k in range(count):
            new = compose((loc[k, 0], loc[k, 1]), (suf[0], suf[1]))
            fin[k, 0], fin[k, 1] = new

    def results(entering):
        entering = right_form(entering)
        for k in range(count):
            mixed = product(left_form(fin[k, 0]), entering)
            o_ref[k] = product_tr(left_form(mixed), right_form_tr(fin[k, 0])) + fin[k, 1]

    @pl.when(quarter == 3)
    def _():
        pack(out_state, congruence(total_e[...], total_l[...], t_ref[...]))
        send_state.start()
        extend_suffix(last - 1)
        finals()
        results(t_ref[...])
        send_state.wait_send()

    @pl.when(quarter == 2)
    def _():
        extend_suffix(last - 1)
        send_state.wait_recv()
        pass_state.start()
        pass_state.wait_recv()
        pack(out_state, congruence(total_e[...], total_l[...], unpack(state)))
        send_state.start()
        finals()
        results(unpack(state))
        pass_state.wait_send()
        send_state.wait_send()

    @pl.when(quarter == 1)
    def _():
        send_gain.start()
        pack(out_state, total_l[...])
        send_cov.start()
        extend_suffix(last - 1)
        finals()
        relay_state.wait_recv()
        relay_state.start()
        pass_state.start()
        pass_state.wait_recv()
        results(unpack(state))
        pass_state.wait_send()
        send_gain.wait_send()
        send_cov.wait_send()
        relay_state.wait_send()

    @pl.when(quarter == 0)
    def _():
        extend_suffix(last - 1)
        send_gain.wait_recv()
        pass_gain.start()
        send_cov.wait_recv()
        pass_cov.start()
        pass_gain.wait()
        pass_cov.wait()
        suf[0], suf[1] = compose((suf[0], suf[1]), (beyond_e[...], unpack(beyond_l)))
        finals()
        relay_state.wait_recv()
        pass_state.start()
        pass_state.wait_recv()
        results(unpack(state))
        pass_state.wait_send()

    for one in pending:
        one.wait_send()


def solution(mesh):
    groups, nbrs = mesh.shape["grp"], mesh.shape["nbr"]
    levels = (nbrs.bit_length() - 1) + ((groups // 4).bit_length() - 1)
    n_sems = 2 + 4 * (levels - 1) + 6

    def per_device(gains, covs, terminal):
        count, width = gains.shape[0], gains.shape[1]
        pair = (2, width, width)
        packed = (2, width // 2 + PAD, width // 2)
        vmem = pl.BlockSpec(memory_space=pltpu.VMEM)
        return pl.pallas_call(
            functools.partial(kernel, groups, nbrs),
            out_shape=jax.ShapeDtypeStruct(gains.shape, F32),
            in_specs=[vmem] * 3,
            out_specs=vmem,
            scratch_shapes=[
                pltpu.VMEM((levels + 1, 2, width, width), F32),
                pltpu.VMEM((levels, 2) + packed, F32),
                pltpu.VMEM((levels + 1, 2, width, width), F32),
                pltpu.VMEM(pair, F32),
                pltpu.VMEM((count,) + pair, F32),
                pltpu.VMEM((count,) + pair, F32),
                pltpu.VMEM(packed, F32),
                pltpu.VMEM(packed, F32),
                pltpu.VMEM((width, width), F32),
                pltpu.VMEM(packed, F32),
                pltpu.SemaphoreType.DMA((n_sems,)),
                pltpu.SemaphoreType.DMA((n_sems,)),
            ],
            compiler_params=pltpu.CompilerParams(collective_id=0, has_side_effects=True),
        )(gains, covs, terminal)

    placed = P(("grp", "nbr"), None, None)
    return jax.shard_map(
        per_device, mesh=mesh, in_specs=(placed, placed, P()), out_specs=placed, check_vma=False
    )
```

```python
import functools

import jax
import jax.numpy as jnp
from jax import lax
from jax.experimental import pallas as pl
from jax.experimental.pallas import tpu as pltpu
from jax.sharding import PartitionSpec as P

MESH = pl.DeviceIdType.MESH
F32, BF16 = jnp.float32, jnp.bfloat16
PAD = 8
PIECES = 4
LIMIT = 32 << 20
NN = (((1,), (0,)), ((), ()))
NT = (((1,), (1,)), ((), ()))


def halves(a):
    high = a.astype(BF16)
    return high, (a - high.astype(F32)).astype(BF16)


def left_form(a):
    high, low = halves(a)
    return jnp.concatenate([high, high, low], axis=1)


def right_form(b):
    high, low = halves(b)
    return jnp.concatenate([high, low, high], axis=0)


def right_form_tr(b):
    high, low = halves(b)
    return jnp.concatenate([high, low, high], axis=1)


def product(a, b):
    return lax.dot_general(a, b, NN, preferred_element_type=F32)


def product_tr(a, b):
    return lax.dot_general(a, b, NT, preferred_element_type=F32)


def congruence(gain, cov, state):
    mixed = product(left_form(gain), right_form(state))
    return product_tr(left_form(mixed), right_form_tr(gain)) + cov


def compose(first, second):
    gain = product(left_form(first[0]), right_form(second[0]))
    return gain, congruence(first[0], first[1], second[1])


def gain_tree(gains):
    rounds = [gains]
    while len(gains) > 1:
        nxt = [
            product(left_form(gains[i]), right_form(gains[i + 1])) for i in range(0, len(gains) - 1, 2)
        ]
        gains = nxt + gains[len(gains) - len(gains) % 2 :]
        rounds.append(gains)
    return rounds


def cov_tree(rounds, covs):
    for gains in rounds[:-1]:
        nxt = [congruence(gains[i], covs[i], covs[i + 1]) for i in range(0, len(covs) - 1, 2)]
        covs = nxt + covs[len(covs) - len(covs) % 2 :]
    return covs[0]


def pieces(rows):
    base = rows // 8 // PIECES * 8
    starts = [0] + [rows - base * (PIECES - i) for i in range(1, PIECES)]
    return [(a, b - a) for a, b in zip(starts, starts[1:] + [rows])]


def symmetric_masks(half):
    rows = lax.broadcasted_iota(jnp.int32, (half, half), 0)
    columns = lax.broadcasted_iota(jnp.int32, (half, half), 1)
    return rows <= columns, rows == columns


def pack(ref, full):
    half = full.shape[0] // 2
    upper, diagonal = symmetric_masks(half)
    a, b, c = full[:half, :half], full[:half, half:], full[half:, half:]
    ref[0, pl.ds(0, half)] = b
    ref[1, pl.ds(0, half)] = jnp.where(upper, a, c)
    line = jnp.sum(jnp.where(diagonal, c, F32(0)), axis=0, keepdims=True)
    line = jnp.broadcast_to(line, (PAD, half))
    ref[0, pl.ds(half, PAD)] = line
    ref[1, pl.ds(half, PAD)] = line


def unpack(ref):
    half = ref.shape[2]
    upper, diagonal = symmetric_masks(half)
    b, mixed = ref[0, pl.ds(0, half)], ref[1, pl.ds(0, half)]
    line = ref[0, pl.ds(half, 1)]
    mixed_tr = mixed.T
    a = jnp.where(upper, mixed, mixed_tr)
    c = jnp.where(diagonal, line, jnp.where(upper, mixed_tr, mixed))
    return jnp.concatenate(
        [jnp.concatenate([a, b], axis=1), jnp.concatenate([b.T, c], axis=1)], axis=0
    )


def kernel(
    groups, nbrs, g_hbm, c_hbm, t_hbm, fin, entering_ref,
    g_ref, c_ref, t_ref, local_sem, tot_e, tot_l, full_l, suf, loc, state, out_state, beyond_e, beyond_l, ssem, rsem,
):
    count, width = g_ref.shape[0], g_ref.shape[1]
    fetched = [
        pltpu.make_async_copy(src, dst, local_sem.at[i])
        for i, (src, dst) in enumerate(((g_hbm, g_ref), (c_hbm, c_ref), (t_hbm, t_ref)))
    ]
    for one in fetched:
        one.start()
    half = width // 2
    quarter_len = groups // 4
    g, n = lax.axis_index("grp"), lax.axis_index("nbr")
    core = lax.rem(n, 2)
    quarter = g // quarter_len
    mate = (g, n + 1 - 2 * core)
    mine = pl.ds(pl.multiple_of(core * half, half), half)

    levels = []
    step = 1
    while step < nbrs:
        bit = lax.rem(n // step, 2)
        levels.append((bit, (g, n + step * (1 - 2 * bit))))
        step *= 2
    step = 1
    while step < quarter_len:
        bit = lax.rem(g // step, 2)
        levels.append((bit, (g + step * (1 - 2 * bit), n)))
        step *= 2
    last = len(levels)
    down = (lax.rem(g + 3 * quarter_len, groups), n)
    up = (lax.rem(g + quarter_len, groups), n)

    barrier = pltpu.get_barrier_semaphore()
    greeted = [partner for _, partner in levels] + [down, up]
    for other in greeted:
        pl.semaphore_signal(barrier, inc=1, device_id=other, device_id_type=MESH)

    sems = iter(range(ssem.shape[0]))

    def copy(src, dst, to, sem):
        return pltpu.make_async_remote_copy(
            src_ref=src, dst_ref=dst, send_sem=ssem.at[sem], recv_sem=rsem.at[sem],
            device_id=to, device_id_type=MESH,
        )

    plan = []
    for at, (bit, partner) in enumerate(levels):
        moves = []
        for ref, piece in ((tot_e, mine), (tot_l, core)):
            if at == 0:
                out = ref.at[at, bit]
                moves.append((copy(out, out, partner, next(sems)), None))
            else:
                out, came = ref.at[at, bit, piece], ref.at[at, 1 - bit, piece]
                moves.append((copy(out, out, partner, next(sems)), copy(came, came, mate, next(sems))))
        plan.append(moves)

    pending = []

    def start(move):
        move[0].start()
        pending.append(move[0])

    def arrive(move):
        move[0].wait_recv()
        if move[1] is not None:
            move[1].start()
            pending.append(move[1])
            move[1].wait_recv()

    def slot_of(at):
        return levels[at][0] if at < last else 0

    def put_cov(at, cov):
        full_l[at, slot_of(at)] = cov
        if at < last:
            pack(tot_l.at[at, slot_of(at)], cov)

    fetched[0].wait()
    rounds = gain_tree([g_ref[k] for k in range(count)])
    tot_e[0, slot_of(0)] = rounds[-1][0]
    pl.semaphore_wait(barrier, len(greeted))
    start(plan[0][0])
    fetched[1].wait()
    put_cov(0, cov_tree(rounds, [c_ref[k] for k in range(count)]))
    start(plan[0][1])
    fetched[2].wait()

    def extend_suffix(at):
        @pl.when(levels[at][0] == 0)
        def _():
            new = compose((suf[0], suf[1]), (tot_e[at, 1], full_l[at, 1]))
            suf[0], suf[1] = new

    for at, (bit, _) in enumerate(levels):
        arrive(plan[at][0])
        first = left_form(tot_e[at, 0])
        tot_e[at + 1, slot_of(at + 1)] = product(first, right_form(tot_e[at, 1]))
        if at + 1 < last:
            start(plan[at + 1][0])
        arrive(plan[at][1])
        full_l[at, 1 - bit] = unpack(tot_l.at[at, 1 - bit])
        put_cov(at + 1, congruence(tot_e[at, 0], full_l[at, 0], full_l[at, 1]))
        if at + 1 < last:
            start(plan[at + 1][1])
            if at == 0:
                own = (g_ref[count - 1], c_ref[count - 1])
                for k in range(count - 1, 0, -1):
                    if k < count - 1:
                        own = compose((g_ref[k], c_ref[k]), own)
                    loc[k, 0], loc[k, 1] = own
                loc[0, 0], loc[0, 1] = tot_e[0, slot_of(0)], full_l[0, slot_of(0)]
                rows = lax.broadcasted_iota(jnp.int32, (width, width), 0)
                columns = lax.broadcasted_iota(jnp.int32, (width, width), 1)
                suf[0] = jnp.where(rows == columns, F32(1), F32(0))
                suf[1] = jnp.zeros((width, width), F32)
            extend_suffix(at)

    total_e, total_l = tot_e.at[last, 0], full_l.at[last, 0]

    send_gain = copy(total_e.at[mine], beyond_e.at[mine], down, next(sems))
    send_cov = copy(out_state.at[core], beyond_l.at[core], down, next(sems))
    pass_gain = copy(beyond_e.at[mine], beyond_e.at[mine], mate, next(sems))
    pass_cov = copy(beyond_l.at[core], beyond_l.at[core], mate, next(sems))
    send_state, relay_state, pass_state = [], [], []
    for begin, size in pieces(half + PAD):
        rows = pl.ds(begin, size)
        state_sem = next(sems)
        send_state.append(copy(out_state.at[core, rows], state.at[core, rows], down, state_sem))
        relay_state.append(copy(state.at[core, rows], state.at[core, rows], down, state_sem))
        pass_state.append(copy(state.at[core, rows], state.at[core, rows], mate, next(sems)))

    def receive_state(relays):
        for i, move in enumerate(relay_state):
            move.wait_recv()
            if relays:
                move.start()
            pass_state[i].start()
        for move in pass_state:
            move.wait_recv()

    def finals():
        for k in range(count):
            new = compose((loc[k, 0], loc[k, 1]), (suf[0], suf[1]))
            fin[k, 0], fin[k, 1] = new

    @pl.when(quarter == 3)
    def _():
        pack(out_state, congruence(total_e[...], total_l[...], t_ref[...]))
        for move in send_state:
            move.start()
        entering_ref[...] = t_ref[...]
        extend_suffix(last - 1)
        finals()
        for move in send_state:
            move.wait_send()

    @pl.when(quarter == 2)
    def _():
        extend_suffix(last - 1)
        receive_state(False)
        entering_ref[...] = unpack(state)
        pack(out_state, congruence(total_e[...], total_l[...], entering_ref[...]))
        for move in send_state:
            move.start()
        finals()
        for move in pass_state + send_state:
            move.wait_send()

    @pl.when(quarter == 1)
    def _():
        send_gain.start()
        pack(out_state, total_l[...])
        send_cov.start()
        extend_suffix(last - 1)
        finals()
        receive_state(True)
        entering_ref[...] = unpack(state)
        for move in pass_state + relay_state + [send_gain, send_cov]:
            move.wait_send()

    @pl.when(quarter == 0)
    def _():
        extend_suffix(last - 1)
        send_gain.wait_recv()
        pass_gain.start()
        send_cov.wait_recv()
        pass_cov.start()
        pass_gain.wait()
        pass_cov.wait()
        suf[0], suf[1] = compose((suf[0], suf[1]), (beyond_e[...], unpack(beyond_l)))
        finals()
        receive_state(False)
        entering_ref[...] = unpack(state)
        for move in pass_state:
            move.wait_send()

    for one in pending:
        one.wait_send()


def apply_kernel(fin, entering_ref, o_hbm, o_ref, sem):
    count = fin.shape[0]
    entering = right_form(entering_ref[...])
    moves = []
    for k in range(count):
        mixed = product(left_form(fin[k, 0]), entering)
        o_ref[k] = product_tr(left_form(mixed), right_form_tr(fin[k, 0])) + fin[k, 1]
        moves.append(pltpu.make_async_copy(o_ref.at[k], o_hbm.at[k], sem.at[k]))
        moves[-1].start()
    for move in moves:
        move.wait()


def solution(mesh):
    groups, nbrs = mesh.shape["grp"], mesh.shape["nbr"]
    levels = (nbrs.bit_length() - 1) + ((groups // 4).bit_length() - 1)
    n_sems = 2 + 4 * (levels - 1) + 4 + 2 * PIECES

    def per_device(gains, covs, terminal):
        count, width = gains.shape[0], gains.shape[1]
        pair = (2, width, width)
        packed = (2, width // 2 + PAD, width // 2)
        vmem, anywhere = pl.BlockSpec(memory_space=pltpu.VMEM), pl.BlockSpec(memory_space=pl.ANY)
        maps, entering = pl.pallas_call(
            functools.partial(kernel, groups, nbrs),
            out_shape=(
                jax.ShapeDtypeStruct((count,) + pair, F32),
                jax.ShapeDtypeStruct((width, width), F32),
            ),
            in_specs=[pl.BlockSpec(memory_space=pltpu.HBM)] * 3,
            out_specs=(vmem, vmem),
            scratch_shapes=[
                pltpu.VMEM(gains.shape, F32),
                pltpu.VMEM(gains.shape, F32),
                pltpu.VMEM((width, width), F32),
                pltpu.SemaphoreType.DMA((3,)),
                pltpu.VMEM((levels + 1, 2, width, width), F32),
                pltpu.VMEM((levels, 2) + packed, F32),
                pltpu.VMEM((levels + 1, 2, width, width), F32),
                pltpu.VMEM(pair, F32),
                pltpu.VMEM((count,) + pair, F32),
                pltpu.VMEM(packed, F32),
                pltpu.VMEM(packed, F32),
                pltpu.VMEM((width, width), F32),
                pltpu.VMEM(packed, F32),
                pltpu.SemaphoreType.DMA((n_sems,)),
                pltpu.SemaphoreType.DMA((n_sems,)),
            ],
            compiler_params=pltpu.CompilerParams(
                collective_id=0, has_side_effects=True, vmem_limit_bytes=LIMIT
            ),
        )(*[pltpu.with_memory_space_constraint(x, pltpu.HBM) for x in (gains, covs, terminal)])
        return pl.pallas_call(
            apply_kernel,
            out_shape=jax.ShapeDtypeStruct(gains.shape, F32),
            in_specs=[vmem, vmem],
            out_specs=anywhere,
            scratch_shapes=[pltpu.VMEM(gains.shape, F32), pltpu.SemaphoreType.DMA((count,))],
            compiler_params=pltpu.CompilerParams(vmem_limit_bytes=LIMIT),
        )(maps, entering)

    placed = P(("grp", "nbr"), None, None)
    return jax.shard_map(
        per_device, mesh=mesh, in_specs=(placed, placed, P()), out_specs=placed, check_vma=False
    )
```

```python
import functools

import jax
import jax.numpy as jnp
from jax import lax
from jax.experimental import pallas as pl
from jax.experimental.pallas import tpu as pltpu
from jax.sharding import PartitionSpec as P

MESH = pl.DeviceIdType.MESH
F32, BF16 = jnp.float32, jnp.bfloat16
PAD = 8
PIECES = 4
LIMIT = 32 << 20
NN = (((1,), (0,)), ((), ()))
NT = (((1,), (1,)), ((), ()))


def halves(a):
    high = a.astype(BF16)
    return high, (a - high.astype(F32)).astype(BF16)


def left_form(a):
    high, low = halves(a)
    return jnp.concatenate([high, high, low], axis=1)


def right_form(b):
    high, low = halves(b)
    return jnp.concatenate([high, low, high], axis=0)


def right_form_tr(b):
    high, low = halves(b)
    return jnp.concatenate([high, low, high], axis=1)


def product(a, b):
    return lax.dot_general(a, b, NN, preferred_element_type=F32)


def product_tr(a, b):
    return lax.dot_general(a, b, NT, preferred_element_type=F32)


def congruence(gain, cov, state):
    mixed = product(left_form(gain), right_form(state))
    return product_tr(left_form(mixed), right_form_tr(gain)) + cov


def compose(first, second):
    gain = product(left_form(first[0]), right_form(second[0]))
    return gain, congruence(first[0], first[1], second[1])


def gain_tree(gains):
    rounds = [gains]
    while len(gains) > 1:
        nxt = [
            product(left_form(gains[i]), right_form(gains[i + 1])) for i in range(0, len(gains) - 1, 2)
        ]
        gains = nxt + gains[len(gains) - len(gains) % 2 :]
        rounds.append(gains)
    return rounds


def cov_tree(rounds, covs):
    for gains in rounds[:-1]:
        nxt = [congruence(gains[i], covs[i], covs[i + 1]) for i in range(0, len(covs) - 1, 2)]
        covs = nxt + covs[len(covs) - len(covs) % 2 :]
    return covs[0]


def pieces(rows):
    base = rows // 8 // PIECES * 8
    starts = [0] + [rows - base * (PIECES - i) for i in range(1, PIECES)]
    return [(a, b - a) for a, b in zip(starts, starts[1:] + [rows])]


def symmetric_masks(half):
    rows = lax.broadcasted_iota(jnp.int32, (half, half), 0)
    columns = lax.broadcasted_iota(jnp.int32, (half, half), 1)
    return rows <= columns, rows == columns


def pack(ref, full):
    half = full.shape[0] // 2
    upper, diagonal = symmetric_masks(half)
    a, b, c = full[:half, :half], full[:half, half:], full[half:, half:]
    ref[0, pl.ds(0, half)] = b
    ref[1, pl.ds(0, half)] = jnp.where(upper, a, c)
    line = jnp.sum(jnp.where(diagonal, c, F32(0)), axis=0, keepdims=True)
    line = jnp.broadcast_to(line, (PAD, half))
    ref[0, pl.ds(half, PAD)] = line
    ref[1, pl.ds(half, PAD)] = line


def unpack(ref):
    half = ref.shape[2]
    upper, diagonal = symmetric_masks(half)
    b, mixed = ref[0, pl.ds(0, half)], ref[1, pl.ds(0, half)]
    line = ref[0, pl.ds(half, 1)]
    mixed_tr = mixed.T
    a = jnp.where(upper, mixed, mixed_tr)
    c = jnp.where(diagonal, line, jnp.where(upper, mixed_tr, mixed))
    return jnp.concatenate(
        [jnp.concatenate([a, b], axis=1), jnp.concatenate([b.T, c], axis=1)], axis=0
    )


def kernel(
    groups, nbrs, g_hbm, c_hbm, t_hbm, fin, entering_ref,
    g_ref, c_ref, t_ref, local_sem, tot_e, tot_l, full_l, quad_e, quad_l, quad_full, two_e, two_l, suf, loc, state, out_state, beyond_e, beyond_l, ssem, rsem,
):
    count, width = g_ref.shape[0], g_ref.shape[1]
    fetched = [
        pltpu.make_async_copy(src, dst, local_sem.at[i])
        for i, (src, dst) in enumerate(((g_hbm, g_ref), (c_hbm, c_ref), (t_hbm, t_ref)))
    ]
    for one in fetched:
        one.start()
    half = width // 2
    quarter_len = groups // 4
    g, n = lax.axis_index("grp"), lax.axis_index("nbr")
    core = lax.rem(n, 2)
    quarter = g // quarter_len
    mate = (g, n + 1 - 2 * core)
    mine = pl.ds(pl.multiple_of(core * half, half), half)

    bits = []
    step = 1
    while step < nbrs:
        bit = lax.rem(n // step, 2)
        bits.append((bit, (0, step * (1 - 2 * bit))))
        step *= 2
    joint = len(bits) - 1
    step = 1
    while step < quarter_len:
        bit = lax.rem(g // step, 2)
        bits.append((bit, (step * (1 - 2 * bit), 0)))
        step *= 2
    partners = [(g + a, n + b) for _, (a, b) in bits]
    levels = [(bits[i][0], partners[i]) for i in range(joint)]
    levels.append(None)
    levels += [(bits[i][0], partners[i]) for i in range(joint + 2, len(bits))]
    last = len(levels)
    low, high = bits[joint][0], bits[joint + 1][0]
    own_slot = 2 * high + low
    low_slot, high_slot, far_slot = 2 * high + 1 - low, 2 * (1 - high) + low, 2 * (1 - high) + 1 - low
    relay_slot = low_slot + core * (high_slot - low_slot)
    relay_to = (g + (1 - core) * bits[joint + 1][1][0], n + core * bits[joint][1][1])
    down = (lax.rem(g + 3 * quarter_len, groups), n)
    up = (lax.rem(g + quarter_len, groups), n)

    barrier = pltpu.get_barrier_semaphore()
    greeted = partners + [down, up]
    for other in greeted:
        pl.semaphore_signal(barrier, inc=1, device_id=other, device_id_type=MESH)

    sems = iter(range(ssem.shape[0]))

    def copy(src, dst, to, sem):
        return pltpu.make_async_remote_copy(
            src_ref=src, dst_ref=dst, send_sem=ssem.at[sem], recv_sem=rsem.at[sem],
            device_id=to, device_id_type=MESH,
        )

    plan = []
    for at, level in enumerate(levels):
        moves = []
        for ref, quad, piece in ((tot_e, quad_e, mine), (tot_l, quad_l, core)):
            if level is None:
                out = quad.at[own_slot, piece]
                move = [copy(out, out, partners[joint + i], next(sems)) for i in range(2)]
                out = quad.at[relay_slot, piece]
                move.append(copy(out, out, relay_to, next(sems)))
                for slot in (low_slot, high_slot, far_slot):
                    out = quad.at[slot, piece]
                    move.append(copy(out, out, mate, next(sems)))
                moves.append(move)
                continue
            bit, partner = level
            if at == 0:
                out = ref.at[at, bit]
                moves.append((copy(out, out, partner, next(sems)), None))
            else:
                out, came = ref.at[at, bit, piece], ref.at[at, 1 - bit, piece]
                moves.append((copy(out, out, partner, next(sems)), copy(came, came, mate, next(sems))))
        plan.append(moves)

    pending = []

    def start(at, what):
        if at < last:
            for one in plan[at][what][: 2 if levels[at] is None else 1]:
                one.start()
                pending.append(one)

    def go(one):
        one.start()
        pending.append(one)

    def arrive(move):
        move[0].wait_recv()
        if move[1] is not None:
            go(move[1])
            move[1].wait_recv()

    def arrive_near(move):
        move[0].wait_recv()
        move[1].wait_recv()
        for one in move[2:5]:
            go(one)
        for one in move[3:5]:
            one.wait_recv()

    def arrive_far(move):
        move[2].wait_recv()
        go(move[5])
        move[5].wait_recv()

    def put_gain(at, gain):
        if at < last and levels[at] is None:
            quad_e[own_slot] = gain
        else:
            tot_e[at, levels[at][0] if at < last else 0] = gain

    def put_cov(at, cov):
        if at < last and levels[at] is None:
            quad_full[own_slot] = cov
            pack(quad_l.at[own_slot], cov)
        elif at < last:
            full_l[at, levels[at][0]] = cov
            pack(tot_l.at[at, levels[at][0]], cov)
        else:
            full_l[at, 0] = cov

    fetched[0].wait()
    rounds = gain_tree([g_ref[k] for k in range(count)])
    put_gain(0, rounds[-1][0])
    loc[0, 0] = rounds[-1][0]
    pl.semaphore_wait(barrier, len(greeted))
    start(0, 0)
    fetched[1].wait()
    cov = cov_tree(rounds, [c_ref[k] for k in range(count)])
    put_cov(0, cov)
    loc[0, 1] = cov
    start(0, 1)
    fetched[2].wait()

    def local_suffixes():
        own = (g_ref[count - 1], c_ref[count - 1])
        for k in range(count - 1, 0, -1):
            if k < count - 1:
                own = compose((g_ref[k], c_ref[k]), own)
            loc[k, 0], loc[k, 1] = own
        rows = lax.broadcasted_iota(jnp.int32, (width, width), 0)
        columns = lax.broadcasted_iota(jnp.int32, (width, width), 1)
        suf[0] = jnp.where(rows == columns, F32(1), F32(0))
        suf[1] = jnp.zeros((width, width), F32)

    def lengthen(bit, gain_ref, cov_ref):
        @pl.when(bit == 0)
        def _():
            suf[0], suf[1] = compose((suf[0], suf[1]), (gain_ref[...], cov_ref[...]))

    def extend_suffix(at):
        if levels[at] is None:
            lengthen(low, quad_e.at[2 * high + 1], quad_full.at[2 * high + 1])
            lengthen(high, two_e.at[1], two_l.at[1])
        else:
            lengthen(levels[at][0], tot_e.at[at, 1], full_l.at[at, 1])

    def pair_gain(which):
        two_e[which] = product(left_form(quad_e[2 * which]), right_form(quad_e[2 * which + 1]))

    def pair_cov(which):
        two_l[which] = congruence(quad_e[2 * which], quad_full[2 * which], quad_full[2 * which + 1])

    for at, level in enumerate(levels):
        if level is None:
            gain_moves, cov_moves = plan[at]
            arrive_near(gain_moves)
            pair_gain(high)
            arrive_near(cov_moves)
            for slot in (low_slot, high_slot):
                quad_full[slot] = unpack(quad_l.at[slot])
            pair_cov(high)
            arrive_far(gain_moves)
            pair_gain(1 - high)
            put_gain(at + 1, product(left_form(two_e[0]), right_form(two_e[1])))
            start(at + 1, 0)
            arrive_far(cov_moves)
            quad_full[far_slot] = unpack(quad_l.at[far_slot])
            pair_cov(1 - high)
            put_cov(at + 1, congruence(two_e[0], two_l[0], two_l[1]))
        else:
            arrive(plan[at][0])
            put_gain(at + 1, product(left_form(tot_e[at, 0]), right_form(tot_e[at, 1])))
            start(at + 1, 0)
            arrive(plan[at][1])
            full_l[at, 1 - level[0]] = unpack(tot_l.at[at, 1 - level[0]])
            put_cov(at + 1, congruence(tot_e[at, 0], full_l[at, 0], full_l[at, 1]))
        start(at + 1, 1)
        if at + 1 < last:
            if at == 0:
                local_suffixes()
            extend_suffix(at)

    total_e, total_l = tot_e.at[last, 0], full_l.at[last, 0]

    send_gain = copy(total_e.at[mine], beyond_e.at[mine], down, next(sems))
    send_cov = copy(out_state.at[core], beyond_l.at[core], down, next(sems))
    pass_gain = copy(beyond_e.at[mine], beyond_e.at[mine], mate, next(sems))
    pass_cov = copy(beyond_l.at[core], beyond_l.at[core], mate, next(sems))
    send_state, relay_state, pass_state = [], [], []
    for begin, size in pieces(half + PAD):
        rows = pl.ds(begin, size)
        state_sem = next(sems)
        send_state.append(copy(out_state.at[core, rows], state.at[core, rows], down, state_sem))
        relay_state.append(copy(state.at[core, rows], state.at[core, rows], down, state_sem))
        pass_state.append(copy(state.at[core, rows], state.at[core, rows], mate, next(sems)))

    def receive_state(relays):
        for i, move in enumerate(relay_state):
            move.wait_recv()
            if relays:
                move.start()
            pass_state[i].start()
        for move in pass_state:
            move.wait_recv()

    def finals():
        for k in range(count):
            new = compose((loc[k, 0], loc[k, 1]), (suf[0], suf[1]))
            fin[k, 0], fin[k, 1] = new

    @pl.when(quarter == 3)
    def _():
        pack(out_state, congruence(total_e[...], total_l[...], t_ref[...]))
        for move in send_state:
            move.start()
        entering_ref[...] = t_ref[...]
        extend_suffix(last - 1)
        finals()
        for move in send_state:
            move.wait_send()

    @pl.when(quarter == 2)
    def _():
        extend_suffix(last - 1)
        receive_state(False)
        entering_ref[...] = unpack(state)
        pack(out_state, congruence(total_e[...], total_l[...], entering_ref[...]))
        for move in send_state:
            move.start()
        finals()
        for move in pass_state + send_state:
            move.wait_send()

    @pl.when(quarter == 1)
    def _():
        send_gain.start()
        pack(out_state, total_l[...])
        send_cov.start()
        extend_suffix(last - 1)
        finals()
        receive_state(True)
        entering_ref[...] = unpack(state)
        for move in pass_state + relay_state + [send_gain, send_cov]:
            move.wait_send()

    @pl.when(quarter == 0)
    def _():
        extend_suffix(last - 1)
        send_gain.wait_recv()
        pass_gain.start()
        send_cov.wait_recv()
        pass_cov.start()
        pass_gain.wait()
        pass_cov.wait()
        suf[0], suf[1] = compose((suf[0], suf[1]), (beyond_e[...], unpack(beyond_l)))
        finals()
        receive_state(False)
        entering_ref[...] = unpack(state)
        for move in pass_state:
            move.wait_send()

    for one in pending:
        one.wait_send()


def apply_kernel(fin, entering_ref, o_hbm, o_ref, sem):
    count = fin.shape[0]
    entering = right_form(entering_ref[...])
    moves = []
    for k in range(count):
        mixed = product(left_form(fin[k, 0]), entering)
        o_ref[k] = product_tr(left_form(mixed), right_form_tr(fin[k, 0])) + fin[k, 1]
        moves.append(pltpu.make_async_copy(o_ref.at[k], o_hbm.at[k], sem.at[k]))
        moves[-1].start()
    for move in moves:
        move.wait()


def solution(mesh):
    groups, nbrs = mesh.shape["grp"], mesh.shape["nbr"]
    levels = (nbrs.bit_length() - 1) + ((groups // 4).bit_length() - 1) - 1
    n_sems = 2 + 4 * (levels - 2) + 12 + 4 + 2 * PIECES

    def per_device(gains, covs, terminal):
        count, width = gains.shape[0], gains.shape[1]
        pair = (2, width, width)
        packed = (2, width // 2 + PAD, width // 2)
        vmem, anywhere = pl.BlockSpec(memory_space=pltpu.VMEM), pl.BlockSpec(memory_space=pl.ANY)
        maps, entering = pl.pallas_call(
            functools.partial(kernel, groups, nbrs),
            out_shape=(
                jax.ShapeDtypeStruct((count,) + pair, F32),
                jax.ShapeDtypeStruct((width, width), F32),
            ),
            in_specs=[pl.BlockSpec(memory_space=pltpu.HBM)] * 3,
            out_specs=(vmem, vmem),
            scratch_shapes=[
                pltpu.VMEM(gains.shape, F32),
                pltpu.VMEM(gains.shape, F32),
                pltpu.VMEM((width, width), F32),
                pltpu.SemaphoreType.DMA((3,)),
                pltpu.VMEM((levels + 1, 2, width, width), F32),
                pltpu.VMEM((levels, 2) + packed, F32),
                pltpu.VMEM((levels + 1, 2, width, width), F32),
                pltpu.VMEM((4, width, width), F32),
                pltpu.VMEM((4,) + packed, F32),
                pltpu.VMEM((4, width, width), F32),
                pltpu.VMEM(pair, F32),
                pltpu.VMEM(pair, F32),
                pltpu.VMEM(pair, F32),
                pltpu.VMEM((count,) + pair, F32),
                pltpu.VMEM(packed, F32),
                pltpu.VMEM(packed, F32),
                pltpu.VMEM((width, width), F32),
                pltpu.VMEM(packed, F32),
                pltpu.SemaphoreType.DMA((n_sems,)),
                pltpu.SemaphoreType.DMA((n_sems,)),
            ],
            compiler_params=pltpu.CompilerParams(
                collective_id=0, has_side_effects=True, vmem_limit_bytes=LIMIT
            ),
        )(*[pltpu.with_memory_space_constraint(x, pltpu.HBM) for x in (gains, covs, terminal)])
        return pl.pallas_call(
            apply_kernel,
            out_shape=jax.ShapeDtypeStruct(gains.shape, F32),
            in_specs=[vmem, vmem],
            out_specs=anywhere,
            scratch_shapes=[pltpu.VMEM(gains.shape, F32), pltpu.SemaphoreType.DMA((count,))],
            compiler_params=pltpu.CompilerParams(vmem_limit_bytes=LIMIT),
        )(maps, entering)

    placed = P(("grp", "nbr"), None, None)
    return jax.shard_map(
        per_device, mesh=mesh, in_specs=(placed, placed, P()), out_specs=placed, check_vma=False
    )
```

```python
import functools

import jax
import jax.numpy as jnp
from jax import lax
from jax.experimental import pallas as pl
from jax.experimental.pallas import tpu as pltpu
from jax.sharding import PartitionSpec as P

MESH = pl.DeviceIdType.MESH
F32, BF16 = jnp.float32, jnp.bfloat16
PAD = 8
PIECES = 4
LIMIT = 32 << 20
NN = (((1,), (0,)), ((), ()))
NT = (((1,), (1,)), ((), ()))


def halves(a):
    high = a.astype(BF16)
    return high, (a - high.astype(F32)).astype(BF16)


def left_form(a):
    high, low = halves(a)
    return jnp.concatenate([high, high, low], axis=1)


def right_form(b):
    high, low = halves(b)
    return jnp.concatenate([high, low, high], axis=0)


def right_form_tr(b):
    high, low = halves(b)
    return jnp.concatenate([high, low, high], axis=1)


def product(a, b):
    return lax.dot_general(a, b, NN, preferred_element_type=F32)


def product_tr(a, b):
    return lax.dot_general(a, b, NT, preferred_element_type=F32)


def congruence(gain, cov, state):
    mixed = product(left_form(gain), right_form(state))
    return product_tr(left_form(mixed), right_form_tr(gain)) + cov


def compose(first, second):
    gain = product(left_form(first[0]), right_form(second[0]))
    return gain, congruence(first[0], first[1], second[1])


def gain_tree(gains):
    rounds = [gains]
    while len(gains) > 1:
        nxt = [
            product(left_form(gains[i]), right_form(gains[i + 1])) for i in range(0, len(gains) - 1, 2)
        ]
        gains = nxt + gains[len(gains) - len(gains) % 2 :]
        rounds.append(gains)
    return rounds


def cov_tree(rounds, covs):
    for gains in rounds[:-1]:
        nxt = [congruence(gains[i], covs[i], covs[i + 1]) for i in range(0, len(covs) - 1, 2)]
        covs = nxt + covs[len(covs) - len(covs) % 2 :]
    return covs[0]


def pieces(rows):
    base = rows // 8 // PIECES * 8
    starts = [0] + [rows - base * (PIECES - i) for i in range(1, PIECES)]
    return [(a, b - a) for a, b in zip(starts, starts[1:] + [rows])]


def symmetric_masks(half):
    rows = lax.broadcasted_iota(jnp.int32, (half, half), 0)
    columns = lax.broadcasted_iota(jnp.int32, (half, half), 1)
    return rows <= columns, rows == columns


def pack(ref, full):
    half = full.shape[0] // 2
    upper, diagonal = symmetric_masks(half)
    a, b, c = full[:half, :half], full[:half, half:], full[half:, half:]
    ref[0, pl.ds(0, half)] = b
    ref[1, pl.ds(0, half)] = jnp.where(upper, a, c)
    line = jnp.sum(jnp.where(diagonal, c, F32(0)), axis=0, keepdims=True)
    line = jnp.broadcast_to(line, (PAD, half))
    ref[0, pl.ds(half, PAD)] = line
    ref[1, pl.ds(half, PAD)] = line


def unpack(ref):
    half = ref.shape[2]
    upper, diagonal = symmetric_masks(half)
    b, mixed = ref[0, pl.ds(0, half)], ref[1, pl.ds(0, half)]
    line = ref[0, pl.ds(half, 1)]
    mixed_tr = mixed.T
    a = jnp.where(upper, mixed, mixed_tr)
    c = jnp.where(diagonal, line, jnp.where(upper, mixed_tr, mixed))
    return jnp.concatenate(
        [jnp.concatenate([a, b], axis=1), jnp.concatenate([b.T, c], axis=1)], axis=0
    )


def kernel(
    groups, nbrs, g_hbm, c_hbm, t_hbm, fin, entering_ref,
    g_ref, c_ref, t_ref, local_sem, tot_e, tot_l, full_l, quad_e, quad_l, quad_full, two_e, two_l, suf, loc, state, out_state, beyond_e, beyond_l, ssem, rsem,
):
    count, width = g_ref.shape[0], g_ref.shape[1]
    fetched = [
        pltpu.make_async_copy(src, dst, local_sem.at[i])
        for i, (src, dst) in enumerate(((g_hbm, g_ref), (c_hbm, c_ref), (t_hbm, t_ref)))
    ]
    for one in fetched:
        one.start()
    half = width // 2
    quarter_len = groups // 4
    g, n = lax.axis_index("grp"), lax.axis_index("nbr")
    core = lax.rem(n, 2)
    quarter = g // quarter_len
    mate = (g, n + 1 - 2 * core)
    mine = pl.ds(pl.multiple_of(core * half, half), half)

    bits = []
    step = 1
    while step < nbrs:
        bit = lax.rem(n // step, 2)
        bits.append((bit, (0, step * (1 - 2 * bit))))
        step *= 2
    joint = len(bits) - 1
    step = 1
    while step < quarter_len:
        bit = lax.rem(g // step, 2)
        bits.append((bit, (step * (1 - 2 * bit), 0)))
        step *= 2
    partners = [(g + a, n + b) for _, (a, b) in bits]
    levels = [(bits[i][0], partners[i]) for i in range(joint)]
    levels.append(None)
    levels += [(bits[i][0], partners[i]) for i in range(joint + 2, len(bits))]
    last = len(levels)
    low, high = bits[joint][0], bits[joint + 1][0]
    own_slot = 2 * high + low
    low_slot, high_slot, far_slot = 2 * high + 1 - low, 2 * (1 - high) + low, 2 * (1 - high) + 1 - low
    relay_slot = low_slot + core * (high_slot - low_slot)
    relay_to = (g + (1 - core) * bits[joint + 1][1][0], n + core * bits[joint][1][1])
    down = (lax.rem(g + 3 * quarter_len, groups), n)
    up = (lax.rem(g + quarter_len, groups), n)

    barrier = pltpu.get_barrier_semaphore()
    greeted = partners + [down, up]
    for other in greeted:
        pl.semaphore_signal(barrier, inc=1, device_id=other, device_id_type=MESH)

    sems = iter(range(ssem.shape[0]))

    def copy(src, dst, to, sem):
        return pltpu.make_async_remote_copy(
            src_ref=src, dst_ref=dst, send_sem=ssem.at[sem], recv_sem=rsem.at[sem],
            device_id=to, device_id_type=MESH,
        )

    plan = []
    for at, level in enumerate(levels):
        moves = []
        for ref, quad, piece in ((tot_e, quad_e, mine), (tot_l, quad_l, core)):
            if level is None:
                out = quad.at[own_slot, piece]
                move = [copy(out, out, partners[joint + i], next(sems)) for i in range(2)]
                out = quad.at[relay_slot, piece]
                move.append(copy(out, out, relay_to, next(sems)))
                for slot in (low_slot, high_slot, far_slot):
                    out = quad.at[slot, piece]
                    move.append(copy(out, out, mate, next(sems)))
                moves.append(move)
                continue
            bit, partner = level
            if at == 0:
                out = ref.at[at, bit]
                moves.append((copy(out, out, partner, next(sems)), None))
            else:
                out, came = ref.at[at, bit, piece], ref.at[at, 1 - bit, piece]
                moves.append((copy(out, out, partner, next(sems)), copy(came, came, mate, next(sems))))
        plan.append(moves)

    pending = []

    def start(at, what):
        if at < last:
            for one in plan[at][what][: 2 if levels[at] is None else 1]:
                one.start()
                pending.append(one)

    def go(one):
        one.start()
        pending.append(one)

    def arrive(move):
        move[0].wait_recv()
        if move[1] is not None:
            go(move[1])
            move[1].wait_recv()

    def arrive_near(move):
        move[0].wait_recv()
        move[1].wait_recv()
        for one in move[2:5]:
            go(one)
        for one in move[3:5]:
            one.wait_recv()

    def arrive_far(move):
        move[2].wait_recv()
        go(move[5])
        move[5].wait_recv()

    def put_gain(at, gain):
        if at < last and levels[at] is None:
            quad_e[own_slot] = gain
        else:
            tot_e[at, levels[at][0] if at < last else 0] = gain

    def put_cov(at, cov):
        if at < last and levels[at] is None:
            quad_full[own_slot] = cov
            pack(quad_l.at[own_slot], cov)
        elif at < last:
            full_l[at, levels[at][0]] = cov
            pack(tot_l.at[at, levels[at][0]], cov)
        else:
            full_l[at, 0] = cov

    fetched[0].wait()
    rounds = gain_tree([g_ref[k] for k in range(count)])
    put_gain(0, rounds[-1][0])
    loc[0, 0] = rounds[-1][0]
    pl.semaphore_wait(barrier, len(greeted))
    start(0, 0)
    fetched[1].wait()
    cov = cov_tree(rounds, [c_ref[k] for k in range(count)])
    put_cov(0, cov)
    loc[0, 1] = cov
    start(0, 1)
    fetched[2].wait()

    def local_suffixes():
        own = (g_ref[count - 1], c_ref[count - 1])
        for k in range(count - 1, 0, -1):
            if k < count - 1:
                own = compose((g_ref[k], c_ref[k]), own)
            loc[k, 0], loc[k, 1] = own
        rows = lax.broadcasted_iota(jnp.int32, (width, width), 0)
        columns = lax.broadcasted_iota(jnp.int32, (width, width), 1)
        suf[0] = jnp.where(rows == columns, F32(1), F32(0))
        suf[1] = jnp.zeros((width, width), F32)

    def lengthen(bit, gain_ref, cov_ref):
        @pl.when(bit == 0)
        def _():
            suf[0], suf[1] = compose((suf[0], suf[1]), (gain_ref[...], cov_ref[...]))

    def extend_suffix(at):
        if levels[at] is None:
            lengthen(low, quad_e.at[2 * high + 1], quad_full.at[2 * high + 1])
            lengthen(high, two_e.at[1], two_l.at[1])
        else:
            lengthen(levels[at][0], tot_e.at[at, 1], full_l.at[at, 1])

    def apply_early(at):
        if at + 1 == last:
            gain = tot_e[last, 0]
            mixed = product(left_form(gain), right_form(t_ref[...]))
            entering_ref[...] = product_tr(left_form(mixed), right_form_tr(gain))

    def pair_gain(which):
        two_e[which] = product(left_form(quad_e[2 * which]), right_form(quad_e[2 * which + 1]))

    def pair_cov(which):
        two_l[which] = congruence(quad_e[2 * which], quad_full[2 * which], quad_full[2 * which + 1])

    for at, level in enumerate(levels):
        if level is None:
            gain_moves, cov_moves = plan[at]
            arrive_near(gain_moves)
            pair_gain(high)
            arrive_near(cov_moves)
            for slot in (low_slot, high_slot):
                quad_full[slot] = unpack(quad_l.at[slot])
            pair_cov(high)
            arrive_far(gain_moves)
            pair_gain(1 - high)
            put_gain(at + 1, product(left_form(two_e[0]), right_form(two_e[1])))
            start(at + 1, 0)
            apply_early(at)
            arrive_far(cov_moves)
            quad_full[far_slot] = unpack(quad_l.at[far_slot])
            pair_cov(1 - high)
            put_cov(at + 1, congruence(two_e[0], two_l[0], two_l[1]))
        else:
            arrive(plan[at][0])
            put_gain(at + 1, product(left_form(tot_e[at, 0]), right_form(tot_e[at, 1])))
            start(at + 1, 0)
            apply_early(at)
            arrive(plan[at][1])
            full_l[at, 1 - level[0]] = unpack(tot_l.at[at, 1 - level[0]])
            put_cov(at + 1, congruence(tot_e[at, 0], full_l[at, 0], full_l[at, 1]))
        start(at + 1, 1)

    total_e, total_l = tot_e.at[last, 0], full_l.at[last, 0]

    send_gain = copy(total_e.at[mine], beyond_e.at[mine], down, next(sems))
    send_cov = copy(out_state.at[core], beyond_l.at[core], down, next(sems))
    pass_gain = copy(beyond_e.at[mine], beyond_e.at[mine], mate, next(sems))
    pass_cov = copy(beyond_l.at[core], beyond_l.at[core], mate, next(sems))
    send_state, relay_state, pass_state = [], [], []
    for begin, size in pieces(half + PAD):
        rows = pl.ds(begin, size)
        state_sem = next(sems)
        send_state.append(copy(out_state.at[core, rows], state.at[core, rows], down, state_sem))
        relay_state.append(copy(state.at[core, rows], state.at[core, rows], down, state_sem))
        pass_state.append(copy(state.at[core, rows], state.at[core, rows], mate, next(sems)))

    def receive_state(relays):
        for i, move in enumerate(relay_state):
            move.wait_recv()
            if relays:
                move.start()
            pass_state[i].start()
        for move in pass_state:
            move.wait_recv()

    def finals():
        for k in range(count):
            new = compose((loc[k, 0], loc[k, 1]), (suf[0], suf[1]))
            fin[k, 0], fin[k, 1] = new

    @pl.when(quarter == 3)
    def _():
        pack(out_state, entering_ref[...] + total_l[...])
        for move in send_state:
            move.start()

    @pl.when(quarter == 1)
    def _():
        send_gain.start()
        pack(out_state, total_l[...])
        send_cov.start()

    local_suffixes()
    for at in range(last):
        extend_suffix(at)

    @pl.when(quarter == 3)
    def _():
        entering_ref[...] = t_ref[...]
        finals()
        for move in send_state:
            move.wait_send()

    @pl.when(quarter == 2)
    def _():
        receive_state(False)
        entering_ref[...] = unpack(state)
        pack(out_state, congruence(total_e[...], total_l[...], entering_ref[...]))
        for move in send_state:
            move.start()
        finals()
        for move in pass_state + send_state:
            move.wait_send()

    @pl.when(quarter == 1)
    def _():
        finals()
        receive_state(True)
        entering_ref[...] = unpack(state)
        for move in pass_state + relay_state + [send_gain, send_cov]:
            move.wait_send()

    @pl.when(quarter == 0)
    def _():
        send_gain.wait_recv()
        pass_gain.start()
        send_cov.wait_recv()
        pass_cov.start()
        pass_gain.wait()
        pass_cov.wait()
        suf[0], suf[1] = compose((suf[0], suf[1]), (beyond_e[...], unpack(beyond_l)))
        finals()
        receive_state(False)
        entering_ref[...] = unpack(state)
        for move in pass_state:
            move.wait_send()

    for one in pending:
        one.wait_send()


def apply_kernel(fin, entering_ref, o_hbm, o_ref, sem):
    count = fin.shape[0]
    entering = right_form(entering_ref[...])
    moves = []
    for k in range(count):
        mixed = product(left_form(fin[k, 0]), entering)
        o_ref[k] = product_tr(left_form(mixed), right_form_tr(fin[k, 0])) + fin[k, 1]
        moves.append(pltpu.make_async_copy(o_ref.at[k], o_hbm.at[k], sem.at[k]))
        moves[-1].start()
    for move in moves:
        move.wait()


def solution(mesh):
    groups, nbrs = mesh.shape["grp"], mesh.shape["nbr"]
    levels = (nbrs.bit_length() - 1) + ((groups // 4).bit_length() - 1) - 1
    n_sems = 2 + 4 * (levels - 2) + 12 + 4 + 2 * PIECES

    def per_device(gains, covs, terminal):
        count, width = gains.shape[0], gains.shape[1]
        pair = (2, width, width)
        packed = (2, width // 2 + PAD, width // 2)
        vmem, anywhere = pl.BlockSpec(memory_space=pltpu.VMEM), pl.BlockSpec(memory_space=pl.ANY)
        maps, entering = pl.pallas_call(
            functools.partial(kernel, groups, nbrs),
            out_shape=(
                jax.ShapeDtypeStruct((count,) + pair, F32),
                jax.ShapeDtypeStruct((width, width), F32),
            ),
            in_specs=[pl.BlockSpec(memory_space=pltpu.HBM)] * 3,
            out_specs=(vmem, vmem),
            scratch_shapes=[
                pltpu.VMEM(gains.shape, F32),
                pltpu.VMEM(gains.shape, F32),
                pltpu.VMEM((width, width), F32),
                pltpu.SemaphoreType.DMA((3,)),
                pltpu.VMEM((levels + 1, 2, width, width), F32),
                pltpu.VMEM((levels, 2) + packed, F32),
                pltpu.VMEM((levels + 1, 2, width, width), F32),
                pltpu.VMEM((4, width, width), F32),
                pltpu.VMEM((4,) + packed, F32),
                pltpu.VMEM((4, width, width), F32),
                pltpu.VMEM(pair, F32),
                pltpu.VMEM(pair, F32),
                pltpu.VMEM(pair, F32),
                pltpu.VMEM((count,) + pair, F32),
                pltpu.VMEM(packed, F32),
                pltpu.VMEM(packed, F32),
                pltpu.VMEM((width, width), F32),
                pltpu.VMEM(packed, F32),
                pltpu.SemaphoreType.DMA((n_sems,)),
                pltpu.SemaphoreType.DMA((n_sems,)),
            ],
            compiler_params=pltpu.CompilerParams(
                collective_id=0, has_side_effects=True, vmem_limit_bytes=LIMIT
            ),
        )(*[pltpu.with_memory_space_constraint(x, pltpu.HBM) for x in (gains, covs, terminal)])
        return pl.pallas_call(
            apply_kernel,
            out_shape=jax.ShapeDtypeStruct(gains.shape, F32),
            in_specs=[vmem, vmem],
            out_specs=anywhere,
            scratch_shapes=[pltpu.VMEM(gains.shape, F32), pltpu.SemaphoreType.DMA((count,))],
            compiler_params=pltpu.CompilerParams(vmem_limit_bytes=LIMIT),
        )(maps, entering)

    placed = P(("grp", "nbr"), None, None)
    return jax.shard_map(
        per_device, mesh=mesh, in_specs=(placed, placed, P()), out_specs=placed, check_vma=False
    )
```
